512 devices in a mesh: row: 16 (over z, y_lo), col: 32 (over y_hi, x, core).
Axes of the slice: x: 4, y: 8 (y_hi: 4, y_lo: 2; y = y_hi * 2 + y_lo), z: 8, core: 2. Of those that a mesh axis runs over, the one named last changes fastest.
Arguments:
- amplitudes: float32 [1024, 20480], P('col', 'row'), may hold values from -6 to 6
- integrals: float32 [20480, 20480], P('row', 'col'), may hold values from -0.0390625 to 0.0390625
- occ_energy: float32 [64], replicated, may hold values from -1.5 to -0.25
- vir_energy: float32 [256], replicated, may hold values from 0.25 to 1.5
- occ_first: int32 [1024], P('row'), may hold values from 0 to 63
- occ_second: int32 [1024], P('row'), may hold values from 0 to 63
- vir_first: int32 [20480], P('col'), may hold values from 0 to 255
- vir_second: int32 [20480], P('col'), may hold values from 0 to 255
Outputs:
- update: float32 [1024, 20480], P('row', 'col')
The draws below stay inside these ranges and needn't reach their ends.
All inputs are finite; a program needn't handle non-finite values.
Results may differ from the reference program's by a relative error of at most 0.00007.
Values sent between devices are 32-bit elements; how exact they have to be, the bound alone decides.
A program may use at most 64 MiB of HBM per device.

```python
import jax
import jax.numpy as jnp
from jax import lax

NV = 20480
OPAIRS = 1024
NOCC = 64
NVIR = 256


def place_ends(entries, stream_key, smallest, top_value):
    shape = entries.shape
    index_at = [jax.random.randint(jax.random.fold_in(stream_key, axis), (), 0, shape[axis]) for axis in range(len(shape))]
    entries = entries.at[tuple(index_at)].set(smallest)
    longest = shape.index(max(shape))
    index_at[longest] = (index_at[longest] + 1) % shape[longest]
    return entries.at[tuple(index_at)].set(top_value)


def level_of(rng, shape, shards, least, top_value):
    level, own = 1.0, jax.random.fold_in(rng, 6)
    for dim, parts in shards:
        draws = jnp.exp(jax.random.uniform(jax.random.fold_in(own, dim), (parts,), jnp.float32, least / len(shards), top_value / len(shards)))
        level = level * jnp.repeat(draws, shape[dim] // parts).reshape([-1 if axis == dim else 1 for axis in range(len(shape))])
    return level


def normal_values(stream_key, shape, scale, reach, split=(), dtype=jnp.bfloat16):
    loudness = level_of(stream_key, shape, split, -0.22, 0.18) if split else 1.0
    array = jax.random.normal(stream_key, shape, jnp.float32) * scale * loudness
    return jnp.minimum(jnp.maximum(array, -reach), reach).astype(dtype)


def setup_inputs(seed: int = 0) -> dict:
    splits = jax.random.split(jax.random.key(seed), 9)
    return {
        "amplitudes": normal_values(splits[0], (OPAIRS, NV), 1.0, 6.0, ((0, 32), (1, 16)), jnp.float32),
        "integrals": normal_values(splits[1], (NV, NV), NV ** -0.5, 0.0390625, ((0, 16), (1, 32)), jnp.float32),
        "occ_energy": jnp.clip(jax.random.uniform(splits[2], (NOCC,), jnp.float32, -1.5, -0.25), -1.5, -0.25),
        "vir_energy": jnp.clip(jax.random.uniform(splits[3], (NVIR,), jnp.float32, 0.25, 1.5), 0.25, 1.5),
        "occ_first": place_ends(jax.random.randint(splits[4], (OPAIRS,), 0, NOCC), jax.random.fold_in(splits[4], 1), 0, NOCC - 1).astype(jnp.int32),
        "occ_second": place_ends(jax.random.randint(splits[5], (OPAIRS,), 0, NOCC), jax.random.fold_in(splits[5], 1), 0, NOCC - 1).astype(jnp.int32),
        "vir_first": place_ends(jax.random.randint(splits[6], (NV,), 0, NVIR), jax.random.fold_in(splits[6], 1), 0, NVIR - 1).astype(jnp.int32),
        "vir_second": place_ends(jax.random.randint(splits[7], (NV,), 0, NVIR), jax.random.fold_in(splits[7], 1), 0, NVIR - 1).astype(jnp.int32),
    }


def reference(amplitudes, integrals, occ_energy, vir_energy, occ_first, occ_second, vir_first, vir_second):
    ladder = jnp.dot(amplitudes, integrals, preferred_element_type=jnp.float32, precision=lax.Precision.HIGHEST)
    occ_sum = occ_energy[occ_first] + occ_energy[occ_second]
    vir_sum = vir_energy[vir_first] + vir_energy[vir_second]
    denom = vir_sum[None, :] - occ_sum[:, None]
    return ladder / denom
```

```python
import functools

import jax
import jax.numpy as jnp
from jax import lax
from jax.experimental import pallas as pl
from jax.experimental.pallas import tpu as pltpu
from jax.sharding import PartitionSpec as P

MESH = pl.DeviceIdType.MESH
LAG = 2
ORDER = (
    (0, 0), (0, 1), (0, 3), (0, 2), (1, 0), (3, 0), (1, 1), (1, 3),
    (3, 1), (3, 3), (2, 0), (1, 2), (3, 2), (2, 1), (2, 3), (2, 2),
)
STEPS = len(ORDER)
HOPS = 5


def pick(index, values):
    out = index * 0 + values[0]
    for k, value in enumerate(values):
        if value != values[0]:
            out = jnp.where(index == k, value, out)
    return out


def kernel(
    a_hbm, b_hbm, out_ref,
    a_all, b_f32, b_hi, b_lo, part, from_fwd, from_bwd, from_pair,
    own_sem, b_sem, a_send, c_send, a_recv, c_recv, z_send, fwd_recv, bwd_recv, p_send, p_recv,
):
    row, col = lax.axis_index("row"), lax.axis_index("col")
    z, y_lo = row // 2, row % 2
    core, x, y_hi = col % 2, (col // 2) % 4, col // 8

    def at_col(y_to, x_to, core_to):
        return {"row": row, "col": ((y_to % 4) * 4 + x_to % 4) * 2 + core_to}

    x_next, x_prev = at_col(y_hi, x + 1, core), at_col(y_hi, x + 3, core)
    y_next, y_prev = at_col(y_hi + 1, x, core), at_col(y_hi + 3, x, core)
    other_core = at_col(y_hi, x, 1 - core)
    z_next = {"row": ((z + 1) % 8) * 2 + y_lo, "col": col}
    z_prev = {"row": ((z + 7) % 8) * 2 + y_lo, "col": col}
    y_pair = {"row": z * 2 + 1 - y_lo, "col": col}
    everyone = (x_next, x_prev, y_next, y_prev, other_core, z_next, z_prev, y_pair)

    load_b = pltpu.make_async_copy(b_hbm, b_f32, b_sem)
    load_b.start()

    def block_of(dy, dx):
        return ((y_hi + dy) % 4) * 4 + (x + dx) % 4

    own = block_of(0, 0)
    own_copies = [
        pltpu.make_async_copy(a_hbm.at[pl.ds(16 * half, 16), :], a_all.at[own, core, half], own_sem.at[half])
        for half in range(2)
    ]
    for copy in own_copies:
        copy.start()

    barrier = pltpu.get_barrier_semaphore()
    for device in everyone:
        pl.semaphore_signal(barrier, inc=1, device_id=device, device_id_type=MESH)
    pl.semaphore_wait(barrier, len(everyone))

    sent = []

    def move(dy, dx, half, device, number):
        block = block_of(dy, dx)
        mine = (dy, dx) == (0, 0)
        slot = a_all.at[block, core, half]
        return pltpu.make_async_remote_copy(
            src_ref=a_hbm.at[pl.ds(16 * half, 16), :] if mine else slot,
            dst_ref=slot,
            send_sem=a_send.at[number],
            recv_sem=a_recv.at[block, half],
            device_id=device,
            device_id_type=MESH,
        )

    def send(dy, dx, half, device):
        sent.append((dy, dx, half, device, len(sent)))
        move(*sent[-1]).start()

    def to_core(block, half, src):
        return pltpu.make_async_remote_copy(
            src_ref=src,
            dst_ref=a_all.at[block, core, half],
            send_sem=c_send.at[block, half],
            recv_sem=c_recv.at[block, half],
            device_id=other_core,
            device_id_type=MESH,
        )

    def arrive(dy, dx, half):
        block = block_of(dy, dx)
        slot = a_all.at[block, core, half]
        pltpu.make_async_remote_copy(
            src_ref=slot, dst_ref=slot, send_sem=c_send.at[block, half],
            recv_sem=a_recv.at[block, half], device_id=other_core, device_id_type=MESH,
        ).wait_recv()

    def give(dy, dx, half):
        block = block_of(dy, dx)
        to_core(block, half, a_all.at[block, core, half]).start()

    send(0, 0, 0, x_next)
    send(0, 0, 1, x_prev)
    send(0, 0, 0, y_next)
    send(0, 0, 1, y_prev)
    for half in range(2):
        to_core(own, half, a_hbm.at[pl.ds(16 * half, 16), :]).start()
    send(0, 0, 1, x_next)
    send(0, 0, 0, x_prev)
    send(0, 0, 1, y_next)
    send(0, 0, 0, y_prev)

    def both_x(dy, half):
        send(dy, 0, half, x_next)
        send(dy, 0, half, x_prev)
        give(dy, 0, half)

    def step_own_row():
        arrive(0, 1, 1)
        send(0, 1, 1, x_prev)
        give(0, 1, 1)
        arrive(0, 3, 0)
        send(0, 3, 0, x_next)
        give(0, 3, 0)
        arrive(0, 1, 0)
        give(0, 1, 0)
        arrive(0, 3, 1)
        give(0, 3, 1)

    def step_far_x_own_row():
        arrive(1, 0, 1)
        both_x(1, 1)
        send(1, 0, 1, y_prev)
        arrive(3, 0, 0)
        both_x(3, 0)
        send(3, 0, 0, y_next)
        for half in range(2):
            arrive(0, 2, half)
            give(0, 2, half)

    def step_next_rows():
        arrive(1, 0, 0)
        both_x(1, 0)
        arrive(3, 0, 1)
        both_x(3, 1)

    def step_sides_a():
        arrive(1, 1, 1)
        send(1, 1, 1, x_prev)
        give(1, 1, 1)
        arrive(1, 3, 1)
        give(1, 3, 1)
        arrive(3, 3, 0)
        send(3, 3, 0, x_next)
        give(3, 3, 0)
        arrive(3, 1, 0)
        give(3, 1, 0)
        arrive(1, 1, 0)
        give(1, 1, 0)
        arrive(1, 3, 0)
        send(1, 3, 0, x_next)
        give(1, 3, 0)

    def step_sides_b():
        for half in range(2):
            arrive(2, 0, half)
            both_x(2, half)
        arrive(3, 1, 1)
        send(3, 1, 1, x_prev)
        give(3, 1, 1)
        arrive(3, 3, 1)
        give(3, 3, 1)

    def step_far(dy):
        def go():
            for half in range(2):
                arrive(dy, 2, half)
                give(dy, 2, half)
        return go

    def step_last_row():
        arrive(2, 1, 1)
        send(2, 1, 1, x_prev)
        give(2, 1, 1)
        arrive(2, 3, 0)
        send(2, 3, 0, x_next)
        give(2, 3, 0)
        arrive(2, 1, 0)
        give(2, 1, 0)
        arrive(2, 3, 1)
        give(2, 3, 1)

    before = {
        1: step_own_row, 3: step_far_x_own_row, 4: step_next_rows, 6: step_sides_a, 8: step_sides_b,
        11: step_far(1), 12: step_far(3), 13: step_last_row, 15: step_far(2),
    }

    load_b.wait()

    @pl.loop(0, 10)
    def _(tile):
        rows = pl.ds(pl.multiple_of(tile * 128, 128), 128)
        whole = b_f32[rows, :]
        high = whole.astype(jnp.bfloat16)
        b_hi[rows, :] = high
        b_lo[rows, :] = (whole - high.astype(jnp.float32)).astype(jnp.bfloat16)

    for copy in own_copies:
        copy.wait()

    def place(step):
        dy = pick(step, [d for d, _ in ORDER])
        dx = pick(step, [d for _, d in ORDER])
        return dy, dx, block_of(dy, dx)

    def hop_copy(block, kind, device, into, recv):
        return pltpu.make_async_remote_copy(
            src_ref=part.at[block, kind], dst_ref=into.at[block, kind],
            send_sem=z_send.at[block, kind], recv_sem=recv.at[block, kind],
            device_id=device, device_id_type=MESH,
        )

    def pair_copy(block, kind):
        return pltpu.make_async_remote_copy(
            src_ref=part.at[block, kind], dst_ref=from_pair.at[block, kind],
            send_sem=p_send.at[block, kind], recv_sem=p_recv.at[block, kind],
            device_id=y_pair, device_id_type=MESH,
        )

    def steps_to_go(block, kind):
        z_to = block // 2
        return (z_to - z + 8) % 8 if kind == 0 else (z - z_to + 8) % 8

    def act(step, stage):
        valid = (step >= 0) & (step < STEPS)
        step = jnp.clip(step, 0, STEPS - 1)
        dy, dx, block = place(step)
        pair_first = dy == 2
        home_pair = block % 2 == y_lo

        if stage == 0:
            @pl.when(valid & pair_first & ~home_pair)
            def _():
                for kind in range(2):
                    pair_copy(block, kind).start()

        for kind in range(2):
            togo = steps_to_go(block, kind)
            hop = jnp.where(togo <= 4, 4 - togo, togo - 5)
            mine = valid & jnp.where(pair_first, home_pair & (hop + 1 == stage), hop == stage)
            ahead, behind = (z_next, z_prev) if kind == 0 else (z_prev, z_next)

            @pl.when(mine)
            def _():
                if stage >= 1:
                    @pl.when(pair_first)
                    def _():
                        pair_copy(block, kind).wait_recv()
                        part[block, kind] = part[block, kind] + from_pair[block, kind]

                    @pl.when(togo <= 3)
                    def _():
                        hop_copy(block, kind, ahead, from_fwd, fwd_recv).wait_recv()
                        part[block, kind] = part[block, kind] + from_fwd[block, kind]

                    @pl.when((togo == 0) | (togo >= 6))
                    def _():
                        hop_copy(block, kind, behind, from_bwd, bwd_recv).wait_recv()
                        part[block, kind] = part[block, kind] + from_bwd[block, kind]

                @pl.when((togo >= 1) & (togo <= 4))
                def _():
                    hop_copy(block, kind, ahead, from_fwd, fwd_recv).start()

                @pl.when(togo >= 5)
                def _():
                    hop_copy(block, kind, behind, from_bwd, bwd_recv).start()

                if stage >= 4:
                    @pl.when((togo == 0) & ~pair_first & ~home_pair)
                    def _():
                        pair_copy(block, kind).start()

    def body(step, carry):
        for when, go in before.items():
            pl.when(step == when)(go)

        @pl.when(step < STEPS)
        def _():
            _, _, block = place(jnp.minimum(step, STEPS - 1))
            for half in range(2):
                slot = a_all.at[block, 1 - core, half]
                pltpu.make_async_remote_copy(
                    src_ref=slot, dst_ref=slot, send_sem=c_send.at[block, half],
                    recv_sem=c_recv.at[block, half], device_id=other_core, device_id_type=MESH,
                ).wait_recv()
            whole = a_all[block].reshape(64, 1280)
            high = whole.astype(jnp.bfloat16)
            low = (whole - high.astype(jnp.float32)).astype(jnp.bfloat16)
            dot = functools.partial(jnp.dot, preferred_element_type=jnp.float32)
            total = dot(high, b_lo[...]) + dot(low, b_hi[...]) + dot(high, b_hi[...])
            part[block] = total.reshape(2, 32, 640)

        act(step, 0)
        for stage in range(HOPS, 0, -1):
            act(step - LAG * stage, stage)
        return carry

    lax.fori_loop(0, STEPS + LAG * HOPS, body, 0)

    own_dy = (row // 4 - y_hi + 4) % 4

    @pl.when(own_dy != 2)
    def _():
        for kind in range(2):
            pair_copy(row, kind).wait_recv()
            part[row, kind] = part[row, kind] + from_pair[row, kind]

    out_ref[...] = part[row].reshape(64, 640)

    for one in sent:
        move(*one).wait_send()

    @pl.loop(0, STEPS)
    def _(block):
        pair_first = (block // 4 - y_hi + 4) % 4 == 2
        home_pair = block % 2 == y_lo
        for half in range(2):
            to_core(block, half, a_all.at[block, core, half]).wait_send()
        for kind in range(2):
            togo = steps_to_go(block, kind)

            @pl.when((togo != 0) & (home_pair | ~pair_first))
            def _():
                hop_copy(block, kind, z_next, from_fwd, fwd_recv).wait_send()

            @pl.when(~home_pair & (pair_first | (togo == 0)))
            def _():
                pair_copy(block, kind).wait_send()


def lookup(table, index):
    positions = jnp.arange(table.shape[0], dtype=jnp.int32)
    picked = jnp.where(index[:, None] == positions[None, :], table[None, :], jnp.float32(0.0))
    return jnp.sum(picked, axis=1)


def per_device(
    amplitudes, integrals, occ_energy, vir_energy, occ_first, occ_second, vir_first, vir_second
):
    dma = pltpu.SemaphoreType.DMA
    f32, bf16 = jnp.float32, jnp.bfloat16
    chunk = pltpu.VMEM((16, 2, 32, 640), f32)
    ladder = pl.pallas_call(
        kernel,
        out_shape=jax.ShapeDtypeStruct((64, 640), f32),
        in_specs=[pl.BlockSpec(memory_space=pl.ANY)] * 2,
        out_specs=pl.BlockSpec(memory_space=pltpu.VMEM),
        scratch_shapes=[
            pltpu.VMEM((16, 2, 2, 16, 1280), f32),
            pltpu.VMEM((1280, 640), f32),
            pltpu.VMEM((1280, 640), bf16),
            pltpu.VMEM((1280, 640), bf16),
            chunk, chunk, chunk, chunk,
            dma((2,)), dma, dma((30,)), dma((16, 2)),
            dma((16, 2)), dma((16, 2)),
            dma((16, 2)), dma((16, 2)), dma((16, 2)), dma((16, 2)), dma((16, 2)),
        ],
        compiler_params=pltpu.CompilerParams(
            collective_id=0, has_side_effects=True, vmem_limit_bytes=60 * 1024 * 1024
        ),
    )(amplitudes, integrals)
    occ_sum = lookup(occ_energy, occ_first) + lookup(occ_energy, occ_second)
    vir_sum = lookup(vir_energy, vir_first) + lookup(vir_energy, vir_second)
    denom = vir_sum[None, :] - occ_sum[:, None]
    return ladder / denom


def solution(mesh):
    placed = (P("col", "row"), P("row", "col"), P(), P(), P("row"), P("row"), P("col"), P("col"))
    return jax.shard_map(
        per_device, mesh=mesh, in_specs=placed, out_specs=P("row", "col"), check_vma=False
    )
```

```python
import functools

import jax
import jax.numpy as jnp
from jax import lax
from jax.experimental import pallas as pl
from jax.experimental.pallas import tpu as pltpu
from jax.sharding import PartitionSpec as P

MESH = pl.DeviceIdType.MESH
ORDER = (
    (0, 0), (0, 1), (0, 3), (0, 2), (1, 0), (3, 0), (1, 3), (3, 3), (1, 1), (3, 1), (2, 0), (3, 2),
    (1, 2), (2, 3), (2, 1), (2, 2),
)
PAIR_FIRST = ((2, 0), (2, 1), (2, 3), (2, 2),)
AROUND = ((0, 0), (0, 1), (0, 3), (0, 2), (1, 0), (3, 0),)
EVENTS = (
    (),
    ((1, 0, 0), (2, 0, 0), (0, 3, 0), (0, 1, 0), (0, 1, 1), (0, 3, 1), (0, 12, 0), (0, 4, 0), (1, 0, 1), (2,
     0, 1)),
    (),
    ((0, 2, 0), (1, 1, 0), (2, 1, 0), (1, 3, 0), (2, 3, 0), (0, 2, 1), (1, 0, 2), (2, 0, 2), (0, 4, 1), (0,
     12, 1)),
    ((0, 7, 0), (0, 15, 0), (1, 1, 1), (2, 1, 1), (1, 3, 1), (2, 3, 1)),
    (),
    ((1, 2, 0), (2, 2, 0), (0, 5, 0), (0, 13, 0), (1, 0, 3), (2, 0, 3), (2, 4, 0), (1, 12, 0), (2, 12, 0), (1,
     4, 0), (0, 8, 0), (0, 7, 1), (0, 15, 1), (1, 1, 2), (2, 1, 2), (1, 3, 2), (2, 3, 2), (1, 2, 1), (2, 2,
     1), (0, 13, 1), (0, 5, 1), (1, 0, 4), (2, 0, 4), (2, 4, 1), (1, 12, 1)),
    (),
    ((0, 8, 1), (2, 12, 1), (1, 4, 1), (2, 7, 0), (1, 15, 0), (1, 7, 0), (2, 15, 0)),
    (),
    ((0, 9, 0), (0, 6, 0), (0, 14, 0), (1, 13, 0), (2, 5, 0), (1, 5, 0), (2, 13, 0)),
    ((1, 1, 3), (1, 3, 3), (2, 1, 3), (2, 3, 3), (2, 2, 2), (1, 2, 2), (1, 12, 2), (1, 0, 5), (2, 4, 2), (2,
     0, 5), (1, 8, 0), (2, 8, 0), (2, 12, 2), (0, 11, 0), (1, 4, 2), (2, 7, 1), (1, 15, 1), (2, 15, 1), (1, 7,
     1), (0, 14, 1), (0, 6, 1), (2, 5, 1), (1, 13, 1), (0, 11, 1), (1, 1, 4), (2, 1, 4), (1, 5, 1), (2, 13,
     1), (1, 3, 4), (0, 9, 1), (2, 3, 4)),
    (),
    ((1, 8, 1), (1, 12, 3), (2, 4, 3), (2, 0, 6), (1, 0, 6), (2, 6, 0), (1, 6, 0), (1, 14, 0), (2, 14, 0), (2,
     8, 1), (2, 12, 3), (1, 4, 3)),
    ((2, 2, 3), (1, 2, 3)),
    ((2, 15, 2), (1, 7, 2), (0, 10, 0), (2, 7, 2), (1, 15, 2), (1, 11, 0), (2, 11, 0), (1, 9, 0), (2, 9, 0),
     (1, 1, 5), (2, 1, 5), (1, 3, 5), (2, 3, 5), (1, 13, 2), (2, 5, 2), (1, 5, 2), (2, 13, 2), (0, 10, 1), (2,
     0, 7), (1, 0, 7), (1, 8, 2), (2, 4, 4), (1, 12, 4), (2, 6, 1), (2, 8, 2), (1, 14, 1), (1, 2, 4), (2, 2,
     4), (1, 6, 1), (2, 12, 4), (2, 14, 1), (2, 15, 3), (1, 7, 3), (1, 4, 4)),
    ((1, 10, 0), (2, 10, 0), (1, 11, 1), (1, 5, 3), (2, 13, 3), (2, 11, 1), (1, 9, 1), (2, 1, 6), (1, 1, 6),
     (2, 7, 3), (1, 15, 3), (2, 3, 6), (2, 9, 1), (1, 3, 6), (2, 4, 5), (1, 12, 5), (2, 2, 5), (1, 2, 5), (1,
     8, 3), (2, 12, 5), (1, 4, 5), (2, 8, 3), (2, 15, 4), (1, 13, 3), (2, 5, 3), (1, 7, 4), (2, 14, 2), (1, 6,
     2), (1, 10, 1), (2, 6, 2), (1, 14, 2), (2, 10, 1), (1, 11, 2), (2, 11, 2), (1, 5, 4), (2, 13, 4), (2, 1,
     7), (1, 9, 2), (2, 7, 4), (1, 15, 4), (2, 3, 7), (2, 9, 2), (1, 1, 7), (1, 3, 7), (2, 2, 6), (1, 2, 6),
     (1, 8, 4), (2, 12, 6), (1, 13, 4), (2, 5, 4), (1, 4, 6), (2, 8, 4), (1, 12, 6), (2, 4, 6), (1, 10, 2),
     (2, 14, 3), (1, 6, 3), (2, 6, 3), (1, 11, 3), (2, 10, 2), (1, 14, 3), (2, 11, 3), (2, 2, 7), (1, 2, 7),
     (1, 9, 3), (2, 9, 3), (1, 8, 5), (2, 8, 5), (1, 12, 7), (2, 4, 7), (2, 12, 7), (1, 10, 3), (1, 4, 7), (2,
     14, 4), (2, 10, 3), (2, 6, 4), (1, 14, 4), (1, 11, 4), (1, 6, 4), (2, 11, 4), (1, 9, 4), (2, 9, 4), (1,
     11, 5), (1, 10, 4), (2, 10, 4), (2, 11, 5), (1, 9, 5), (2, 9, 5), (1, 10, 5), (2, 10, 5)),
)
PIECE = 16


def pick(index, values):
    out = index * 0 + values[0]
    for k, value in enumerate(values):
        if value != values[0]:
            out = jnp.where(index == k, value, out)
    return out


def column(line):
    n = line.shape[1]
    down = lax.broadcasted_iota(jnp.int32, (n, n), 0)
    along = lax.broadcasted_iota(jnp.int32, (n, n), 1)
    return jnp.sum(jnp.where(down == along, line, jnp.zeros_like(line)), axis=1, keepdims=True)


def lookup(table, index):
    n, m = table.shape[1], index.shape[1]
    at = lax.broadcasted_iota(jnp.int32, (n, m), 0)
    return jnp.sum(jnp.where(at == index, column(table), jnp.float32(0.0)), axis=0, keepdims=True)


def kernel(
    a_hbm, b_hbm, occ_energy, vir_energy, occ_first, occ_second, vir_first, vir_second, out_ref,
    a_all, b_f32, b_hi, b_lo, part, from_fwd, from_bwd, from_pair, denom,
    own_sem, b_sem, a_send, c_send, a_recv, c_recv, z_send, fwd_recv, bwd_recv, p_send, p_recv,
):
    row, col = lax.axis_index("row"), lax.axis_index("col")
    z, y_lo = row // 2, row % 2
    core, x, y_hi = col % 2, (col // 2) % 4, col // 8

    def at_col(y_to, x_to, core_to):
        return {"row": row, "col": ((y_to % 4) * 4 + x_to % 4) * 2 + core_to}

    x_next, x_prev = at_col(y_hi, x + 1, core), at_col(y_hi, x + 3, core)
    y_next, y_prev = at_col(y_hi + 1, x, core), at_col(y_hi + 3, x, core)
    other_core = at_col(y_hi, x, 1 - core)
    z_next = {"row": ((z + 1) % 8) * 2 + y_lo, "col": col}
    z_prev = {"row": ((z + 7) % 8) * 2 + y_lo, "col": col}
    y_pair = {"row": z * 2 + 1 - y_lo, "col": col}
    everyone = (x_next, x_prev, y_next, y_prev, other_core, z_next, z_prev, y_pair)

    load_b = pltpu.make_async_copy(b_hbm, b_f32, b_sem)

    ys = [(y_hi + d) % 4 for d in range(4)]
    xs = [(x + d) % 4 for d in range(4)]

    def block_of(dy, dx):
        return ys[dy] * 4 + xs[dx]

    def in_hbm(half):
        return a_hbm.at[pl.ds(16 * half, 16), :]

    own = block_of(0, 0)
    own_copies = [
        pltpu.make_async_copy(in_hbm(half), a_all.at[own, core, half], own_sem.at[half]) for half in range(2)
    ]

    barrier = pltpu.get_barrier_semaphore()
    for device in everyone:
        pl.semaphore_signal(barrier, inc=1, device_id=device, device_id_type=MESH)
    for copy in own_copies:
        copy.start()
    load_b.start()
    pl.semaphore_wait(barrier, len(everyone))

    sent = []

    def move(dy, dx, half, device, number):
        block = block_of(dy, dx)
        slot = a_all.at[block, core, half]
        return pltpu.make_async_remote_copy(
            src_ref=in_hbm(half) if (dy, dx) == (0, 0) else slot,
            dst_ref=slot,
            send_sem=a_send.at[number],
            recv_sem=a_recv.at[block, half],
            device_id=device,
            device_id_type=MESH,
        )

    def send(dy, dx, half, device):
        sent.append((dy, dx, half, device, len(sent)))
        move(*sent[-1]).start()

    def to_core(block, half, src):
        return pltpu.make_async_remote_copy(
            src_ref=src,
            dst_ref=a_all.at[block, core, half],
            send_sem=c_send.at[block, half],
            recv_sem=c_recv.at[block, half],
            device_id=other_core,
            device_id_type=MESH,
        )

    def arrive(block, half, whose, recv):
        slot = a_all.at[block, whose, half]
        pltpu.make_async_remote_copy(
            src_ref=slot, dst_ref=slot, send_sem=c_send.at[block, half],
            recv_sem=recv.at[block, half], device_id=other_core, device_id_type=MESH,
        ).wait_recv()

    def gather_event(dy, dx, half):
        block = block_of(dy, dx)
        arrive(block, half, core, a_recv)
        if dx == 0:
            if (dy, half) == (1, 1):
                send(dy, dx, half, y_prev)
            if (dy, half) == (3, 0):
                send(dy, dx, half, y_next)
            send(dy, dx, half, x_prev if half else x_next)
            send(dy, dx, half, x_next if half else x_prev)
        if (dx, half) == (1, 1):
            send(dy, dx, half, x_prev)
        if (dx, half) == (3, 0):
            send(dy, dx, half, x_next)
        to_core(block, half, a_all.at[block, core, half]).start()

    def hop_copy(block, piece, device, into, recv):
        return pltpu.make_async_remote_copy(
            src_ref=part.at[block, piece], dst_ref=into.at[block, piece],
            send_sem=z_send.at[block, piece], recv_sem=recv.at[block, piece],
            device_id=device, device_id_type=MESH,
        )

    def pair_copy(block, piece):
        return pltpu.make_async_remote_copy(
            src_ref=part.at[block, piece], dst_ref=from_pair.at[block, piece],
            send_sem=p_send.at[block, piece], recv_sem=p_recv.at[block, piece],
            device_id=y_pair, device_id_type=MESH,
        )

    def steps_to_go(block, parity):
        return (block // 2 - z + 8) % 8 if parity == 0 else (z - block // 2 + 8) % 8

    def reduce_event(dy, dx, parity, stage):
        block = block_of(dy, dx)
        togo = steps_to_go(block, parity)
        home = block % 2 == y_lo
        pair_first, around = (dy, dx) in PAIR_FIRST, (dy, dx) in AROUND
        ahead, behind = (z_next, z_prev) if parity == 0 else (z_prev, z_next)
        hop = stage - 1 if pair_first else stage

        def on_pieces(do):
            for piece in (parity, parity + 2):
                do(piece)

        if hop < 0:
            @pl.when(~home)
            def _():
                on_pieces(lambda piece: pair_copy(block, piece).start())
            return

        def case(left, fwd_in, bwd_in, device, into, recv):
            @pl.when((togo == left) & home if pair_first else togo == left)
            def _():
                def do(piece):
                    total = []
                    if pair_first:
                        pair_copy(block, piece).wait_recv()
                        total.append(from_pair)
                    if fwd_in:
                        hop_copy(block, piece, ahead, from_fwd, fwd_recv).wait_recv()
                        total.append(from_fwd)
                    if bwd_in:
                        hop_copy(block, piece, behind, from_bwd, bwd_recv).wait_recv()
                        total.append(from_bwd)
                    if total:
                        part[block, piece] = sum((t[block, piece] for t in total), part[block, piece])
                    if device is not None:
                        hop_copy(block, piece, device, into, recv).start()

                on_pieces(do)
                if device is None and not pair_first:
                    @pl.when(~home)
                    def _():
                        on_pieces(lambda piece: pair_copy(block, piece).start())

        if around:
            if hop < 7:
                case(7 - hop, hop > 0, False, ahead, from_fwd, fwd_recv)
            else:
                case(0, True, False, None, None, None)
        elif hop < 4:
            case(4 - hop, hop > 0, False, ahead, from_fwd, fwd_recv)
            if hop < 3:
                case(5 + hop, False, hop > 0, behind, from_bwd, bwd_recv)
        else:
            case(0, True, True, None, None, None)

    send(0, 0, 0, x_next)
    send(0, 0, 1, x_prev)
    send(0, 0, 0, y_next)
    send(0, 0, 1, y_prev)
    send(0, 0, 1, x_next)
    send(0, 0, 0, x_prev)
    send(0, 0, 1, y_next)
    send(0, 0, 0, y_prev)
    for half in range(2):
        to_core(own, half, in_hbm(half)).start()

    vir_sum = lookup(vir_energy[...], vir_first[...]) + lookup(vir_energy[...], vir_second[...])
    occ_sum = lookup(occ_energy[...], occ_first[...]) + lookup(occ_energy[...], occ_second[...])
    denom[...] = vir_sum - column(occ_sum)

    load_b.wait()

    @pl.loop(0, 10)
    def _(tile):
        rows = pl.ds(pl.multiple_of(tile * 128, 128), 128)
        whole = b_f32[rows, :]
        high = whole.astype(jnp.bfloat16)
        b_hi[rows, :] = high
        b_lo[rows, :] = (whole - high.astype(jnp.float32)).astype(jnp.bfloat16)

    for copy in own_copies:
        copy.wait()

    def run_events(events):
        for kind, name, detail in events:
            if kind == 0:
                gather_event(name // 4, name % 4, detail)
            else:
                reduce_event(name // 4, name % 4, kind - 1, detail)

    def body(step, carry):
        for k, events in enumerate(EVENTS):
            if events and k < len(ORDER):
                pl.when(step == k)(functools.partial(run_events, events))
        block = block_at(step)
        for half in range(2):
            arrive(block, half, 1 - core, c_recv)
        whole = a_all[block].reshape(64, 1280)
        high = whole.astype(jnp.bfloat16)
        low = (whole - high.astype(jnp.float32)).astype(jnp.bfloat16)
        dot = functools.partial(jnp.dot, preferred_element_type=jnp.float32)
        both = dot(jnp.concatenate([high, low], axis=0), b_hi[...])
        total = dot(high, b_lo[...]) + both[64:] + both[:64]
        part[block] = total.reshape(64 // PIECE, PIECE, 640)
        return carry

    def block_at(step):
        dy, dx = pick(step, [d for d, _ in ORDER]), pick(step, [d for _, d in ORDER])
        return ((y_hi + dy) % 4) * 4 + (x + dx) % 4

    lax.fori_loop(0, len(ORDER), body, 0)
    run_events(EVENTS[len(ORDER)])

    def is_pair_first(block):
        dy, dx = (block // 4 - y_hi + 4) % 4, (block % 4 - x + 4) % 4
        return functools.reduce(lambda a, b: a | b, [(dy == a) & (dx == b) for a, b in PAIR_FIRST])

    whole_sum = part[row].reshape(64, 640)
    out_ref[...] = whole_sum / denom[...]

    @pl.when(~is_pair_first(row))
    def _():
        for piece in range(64 // PIECE):
            pair_copy(row, piece).wait_recv()
        out_ref[...] = (part[row].reshape(64, 640) + from_pair[row].reshape(64, 640)) / denom[...]

    for one in sent:
        move(*one).wait_send()

    @pl.loop(0, 16)
    def _(block):
        pair_first = is_pair_first(block)
        home = block % 2 == y_lo
        for half in range(2):
            to_core(block, half, a_all.at[block, core, half]).wait_send()
        left = steps_to_go(block, 0)

        @pl.when((left != 0) & (home | ~pair_first))
        def _():
            for piece in range(64 // PIECE):
                hop_copy(block, piece, z_next, from_fwd, fwd_recv).wait_send()

        @pl.when(~home & (pair_first | (left == 0)))
        def _():
            for piece in range(64 // PIECE):
                pair_copy(block, piece).wait_send()


def per_device(
    amplitudes, integrals, occ_energy, vir_energy, occ_first, occ_second, vir_first, vir_second
):
    dma = pltpu.SemaphoreType.DMA
    f32, bf16 = jnp.float32, jnp.bfloat16
    pieces = 64 // PIECE
    chunk = pltpu.VMEM((16, pieces, PIECE, 640), f32)
    small = (occ_energy, vir_energy, occ_first, occ_second, vir_first, vir_second)
    return pl.pallas_call(
        kernel,
        out_shape=jax.ShapeDtypeStruct((64, 640), f32),
        in_specs=[pl.BlockSpec(memory_space=pl.ANY)] * 2 + [pl.BlockSpec(memory_space=pltpu.VMEM)] * 6,
        out_specs=pl.BlockSpec(memory_space=pltpu.VMEM),
        scratch_shapes=[
            pltpu.VMEM((16, 2, 2, 16, 1280), f32),
            pltpu.VMEM((1280, 640), f32),
            pltpu.VMEM((1280, 640), bf16),
            pltpu.VMEM((1280, 640), bf16),
            chunk, chunk, chunk, chunk,
            pltpu.VMEM((64, 640), f32),
            dma((2,)), dma, dma((30,)), dma((16, 2)),
            dma((16, 2)), dma((16, 2)),
            dma((16, pieces)), dma((16, pieces)), dma((16, pieces)), dma((16, pieces)), dma((16, pieces)),
        ],
        compiler_params=pltpu.CompilerParams(
            collective_id=0, has_side_effects=True, vmem_limit_bytes=60 * 1024 * 1024
        ),
    )(amplitudes, integrals, *(array.reshape(1, -1) for array in small))


def solution(mesh):
    placed = (P("col", "row"), P("row", "col"), P(), P(), P("row"), P("row"), P("col"), P("col"))
    return jax.shard_map(
        per_device, mesh=mesh, in_specs=placed, out_specs=P("row", "col"), check_vma=False
    )
```

```python
import functools

import jax
import jax.numpy as jnp
from jax import lax
from jax.experimental import pallas as pl
from jax.experimental.pallas import tpu as pltpu
from jax.sharding import PartitionSpec as P

MESH = pl.DeviceIdType.MESH
ORDER = (
    (0, 0), (0, 1), (0, 3), (0, 2), (1, 0), (3, 0), (2, 0), (3, 3), (1, 1), (1, 3), (3, 1), (2, 3),
    (2, 1), (1, 2), (3, 2), (2, 2),
)
PAIR_FIRST = ((2, 0), (2, 1), (2, 3), (2, 2),)
AROUND = ((0, 0), (0, 1), (0, 3), (0, 2), (1, 0), (3, 0),)
EVENTS = (
    (),
    ((0, 1, 1), (0, 3, 0), (1, 0, 0), (2, 0, 0), (0, 1, 0), (0, 3, 1), (0, 4, 1), (0, 12, 0), (1, 0, 1), (2,
     0, 1)),
    (),
    ((0, 2, 0), (0, 2, 1), (2, 1, 0), (2, 3, 0), (1, 1, 0), (0, 4, 0), (0, 12, 1), (1, 3, 0), (1, 0, 2), (2,
     0, 2)),
    ((1, 2, 0), (0, 5, 1), (0, 7, 1), (2, 2, 0)),
    (),
    ((1, 3, 1), (0, 15, 0), (2, 3, 1), (1, 1, 1), (2, 1, 1), (0, 8, 0), (0, 8, 1), (1, 12, 0), (1, 4, 0), (2,
     4, 0), (2, 12, 0), (0, 13, 0), (2, 2, 1), (1, 0, 3), (1, 2, 1), (0, 7, 0), (0, 15, 1), (0, 5, 0)),
    ((1, 8, 0), (2, 8, 0), (0, 13, 1), (2, 3, 2), (1, 3, 2), (2, 0, 3), (2, 1, 2), (1, 1, 2), (1, 4, 1), (1,
     12, 1), (0, 6, 1), (2, 12, 1)),
    (),
    (),
    (),
    ((1, 5, 0), (2, 7, 0), (2, 4, 1), (2, 5, 0), (1, 15, 0), (2, 0, 4), (1, 0, 4), (2, 2, 2), (1, 7, 0), (1,
     2, 2), (1, 8, 1), (1, 13, 0), (0, 11, 0), (0, 9, 1), (0, 9, 0), (1, 12, 2), (0, 11, 1), (0, 14, 0), (2,
     13, 0), (2, 12, 2), (2, 8, 1), (2, 4, 2), (1, 4, 2), (2, 1, 3), (2, 15, 0), (2, 0, 5), (1, 1, 3), (1, 3,
     3), (2, 3, 3), (1, 0, 5), (1, 5, 1), (0, 6, 0), (0, 14, 1)),
    (),
    ((2, 9, 0), (1, 8, 2), (2, 5, 1), (1, 7, 1), (2, 7, 1), (1, 12, 3), (2, 8, 2), (2, 13, 1), (1, 13, 1), (1,
     9, 0), (2, 11, 0), (1, 2, 3), (0, 10, 1), (2, 2, 3), (0, 10, 0), (1, 11, 0), (2, 12, 3), (2, 4, 3), (2,
     15, 1)),
    (),
    ((1, 3, 4), (1, 1, 4), (1, 0, 6), (2, 3, 4), (2, 1, 4), (1, 15, 1), (1, 4, 3), (2, 0, 6), (2, 5, 2), (1,
     5, 2), (1, 14, 0), (2, 14, 0), (1, 2, 4), (1, 6, 0), (2, 6, 0), (2, 8, 3)),
    ((1, 7, 2), (1, 13, 2), (1, 12, 4), (2, 13, 2), (2, 7, 2), (1, 15, 2), (1, 9, 1), (2, 9, 1), (2, 15, 2),
     (2, 2, 4), (1, 3, 5), (1, 1, 5), (2, 3, 5), (1, 10, 0), (2, 10, 0), (2, 1, 5), (2, 0, 7), (1, 11, 1), (2,
     12, 4), (2, 4, 4), (2, 11, 1), (1, 5, 3), (1, 4, 4), (2, 6, 1), (1, 14, 1), (1, 6, 1), (2, 14, 1), (2, 5,
     3), (2, 2, 5), (1, 7, 3), (2, 13, 3), (1, 2, 5), (2, 15, 3), (2, 4, 5), (1, 12, 5), (2, 8, 4), (1, 10,
     1), (1, 8, 4), (1, 8, 3), (2, 9, 2), (2, 7, 3), (1, 1, 6), (1, 4, 5), (2, 11, 2), (2, 12, 5), (1, 9, 2),
     (2, 1, 6), (2, 3, 6), (2, 10, 1), (1, 11, 2), (1, 5, 4), (1, 13, 3), (1, 3, 6), (1, 14, 2), (1, 15, 3),
     (1, 0, 7), (2, 14, 2), (1, 2, 6), (1, 6, 2), (2, 6, 2), (2, 5, 4), (2, 13, 4), (2, 2, 6), (1, 1, 7), (1,
     7, 4), (2, 1, 7), (2, 8, 5), (1, 12, 6), (2, 12, 6), (1, 14, 3), (1, 10, 2), (1, 3, 7), (1, 8, 5), (2, 3,
     7), (2, 15, 4), (1, 9, 3), (1, 13, 4), (1, 15, 4), (2, 9, 3), (2, 6, 3), (2, 7, 4), (1, 4, 6), (2, 4, 6),
     (2, 11, 3), (1, 2, 7), (2, 2, 7), (1, 11, 3), (2, 10, 2), (2, 14, 3), (1, 6, 3), (2, 4, 7), (1, 10, 3),
     (2, 10, 3), (1, 4, 7), (1, 12, 7), (1, 9, 4), (2, 9, 4), (1, 14, 4), (1, 11, 4), (2, 11, 4), (2, 11, 5),
     (2, 14, 4), (1, 11, 5), (1, 9, 5), (2, 9, 5), (1, 10, 4), (2, 10, 4), (1, 6, 4), (2, 12, 7), (2, 6, 4),
     (1, 10, 5), (2, 10, 5)),
)
PIECE = 16


def pick(index, values):
    out = index * 0 + values[0]
    for k, value in enumerate(values):
        if value != values[0]:
            out = jnp.where(index == k, value, out)
    return out


def column(line):
    n = line.shape[1]
    down = lax.broadcasted_iota(jnp.int32, (n, n), 0)
    along = lax.broadcasted_iota(jnp.int32, (n, n), 1)
    return jnp.sum(jnp.where(down == along, line, jnp.zeros_like(line)), axis=1, keepdims=True)


def lookup(table, index):
    n, m = table.shape[1], index.shape[1]
    at = lax.broadcasted_iota(jnp.int32, (n, m), 0)
    return jnp.sum(jnp.where(at == index, column(table), jnp.float32(0.0)), axis=0, keepdims=True)


def kernel(
    a_hbm, b_hbm, *refs
):
    small_hbm, out_ref, small = refs[:6], refs[6], refs[7:13]
    body_of(a_hbm, b_hbm, small_hbm, out_ref, small, *refs[13:])


def body_of(
    a_hbm, b_hbm, small_hbm, out_ref, small,
    a_all, b_f32, b_hi, b_lo, part, from_fwd, from_bwd, from_pair, denom,
    own_sem, b_sem, small_sem, a_send, c_send, a_recv, c_recv, z_send, fwd_recv, bwd_recv, p_send, p_recv,
):
    row, col = lax.axis_index("row"), lax.axis_index("col")
    z, y_lo = row // 2, row % 2
    core, x, y_hi = col % 2, (col // 2) % 4, col // 8

    def at_col(y_to, x_to, core_to):
        return {"row": row, "col": ((y_to % 4) * 4 + x_to % 4) * 2 + core_to}

    x_next, x_prev = at_col(y_hi, x + 1, core), at_col(y_hi, x + 3, core)
    y_next, y_prev = at_col(y_hi + 1, x, core), at_col(y_hi + 3, x, core)
    other_core = at_col(y_hi, x, 1 - core)
    z_next = {"row": ((z + 1) % 8) * 2 + y_lo, "col": col}
    z_prev = {"row": ((z + 7) % 8) * 2 + y_lo, "col": col}
    y_pair = {"row": z * 2 + 1 - y_lo, "col": col}
    everyone = (x_next, x_prev, y_next, y_prev, other_core, z_next, z_prev, y_pair)

    load_b = pltpu.make_async_copy(b_hbm, b_f32, b_sem)
    load_small = [
        pltpu.make_async_copy(src, dst, small_sem.at[k]) for k, (src, dst) in enumerate(zip(small_hbm, small))
    ]
    occ_energy, vir_energy, occ_first, occ_second, vir_first, vir_second = small

    ys = [(y_hi + d) % 4 for d in range(4)]
    xs = [(x + d) % 4 for d in range(4)]

    def block_of(dy, dx):
        return ys[dy] * 4 + xs[dx]

    def in_hbm(half):
        return a_hbm.at[pl.ds(16 * half, 16), :]

    own = block_of(0, 0)
    own_copies = [
        pltpu.make_async_copy(in_hbm(half), a_all.at[own, core, half], own_sem.at[half]) for half in range(2)
    ]

    barrier = pltpu.get_barrier_semaphore()
    for device in everyone:
        pl.semaphore_signal(barrier, inc=1, device_id=device, device_id_type=MESH)
    for copy in own_copies:
        copy.start()
    for copy in load_small:
        copy.start()
    load_b.start()
    pl.semaphore_wait(barrier, len(everyone))

    sent = []

    def move(dy, dx, half, device, number):
        block = block_of(dy, dx)
        slot = a_all.at[block, core, half]
        return pltpu.make_async_remote_copy(
            src_ref=in_hbm(half) if (dy, dx) == (0, 0) else slot,
            dst_ref=slot,
            send_sem=a_send.at[number],
            recv_sem=a_recv.at[block, half],
            device_id=device,
            device_id_type=MESH,
        )

    def send(dy, dx, half, device):
        sent.append((dy, dx, half, device, len(sent)))
        move(*sent[-1]).start()

    def to_core(block, half, src):
        return pltpu.make_async_remote_copy(
            src_ref=src,
            dst_ref=a_all.at[block, core, half],
            send_sem=c_send.at[block, half],
            recv_sem=c_recv.at[block, half],
            device_id=other_core,
            device_id_type=MESH,
        )

    def arrive(block, half, whose, recv):
        slot = a_all.at[block, whose, half]
        pltpu.make_async_remote_copy(
            src_ref=slot, dst_ref=slot, send_sem=c_send.at[block, half],
            recv_sem=recv.at[block, half], device_id=other_core, device_id_type=MESH,
        ).wait_recv()

    def gather_event(dy, dx, half):
        block = block_of(dy, dx)
        arrive(block, half, core, a_recv)
        if dx == 0:
            if (dy, half) == (1, 1):
                send(dy, dx, half, y_prev)
            if (dy, half) == (3, 0):
                send(dy, dx, half, y_next)
            send(dy, dx, half, x_prev if half else x_next)
            send(dy, dx, half, x_next if half else x_prev)
        if (dx, half) == (1, 1):
            send(dy, dx, half, x_prev)
        if (dx, half) == (3, 0):
            send(dy, dx, half, x_next)
        to_core(block, half, a_all.at[block, core, half]).start()

    def hop_copy(block, piece, device, into, recv):
        return pltpu.make_async_remote_copy(
            src_ref=part.at[block, piece], dst_ref=into.at[block, piece],
            send_sem=z_send.at[block, piece], recv_sem=recv.at[block, piece],
            device_id=device, device_id_type=MESH,
        )

    def pair_copy(block, piece):
        return pltpu.make_async_remote_copy(
            src_ref=part.at[block, piece], dst_ref=from_pair.at[block, piece],
            send_sem=p_send.at[block, piece], recv_sem=p_recv.at[block, piece],
            device_id=y_pair, device_id_type=MESH,
        )

    def steps_to_go(block, parity):
        return (block // 2 - z + 8) % 8 if parity == 0 else (z - block // 2 + 8) % 8

    def reduce_event(dy, dx, parity, stage):
        block = block_of(dy, dx)
        togo = steps_to_go(block, parity)
        home = block % 2 == y_lo
        pair_first, around = (dy, dx) in PAIR_FIRST, (dy, dx) in AROUND
        ahead, behind = (z_next, z_prev) if parity == 0 else (z_prev, z_next)
        hop = stage - 1 if pair_first else stage

        def on_pieces(do):
            for piece in (parity, parity + 2):
                do(piece)

        if hop < 0:
            @pl.when(~home)
            def _():
                on_pieces(lambda piece: pair_copy(block, piece).start())
            return

        def case(left, fwd_in, bwd_in, device, into, recv):
            @pl.when((togo == left) & home if pair_first else togo == left)
            def _():
                def do(piece):
                    total = []
                    if pair_first:
                        pair_copy(block, piece).wait_recv()
                        total.append(from_pair)
                    if fwd_in:
                        hop_copy(block, piece, ahead, from_fwd, fwd_recv).wait_recv()
                        total.append(from_fwd)
                    if bwd_in:
                        hop_copy(block, piece, behind, from_bwd, bwd_recv).wait_recv()
                        total.append(from_bwd)
                    if total:
                        part[block, piece] = sum((t[block, piece] for t in total), part[block, piece])
                    if device is not None:
                        hop_copy(block, piece, device, into, recv).start()

                on_pieces(do)
                if device is None and not pair_first:
                    @pl.when(~home)
                    def _():
                        on_pieces(lambda piece: pair_copy(block, piece).start())

        if around:
            if hop < 7:
                case(7 - hop, hop > 0, False, ahead, from_fwd, fwd_recv)
            else:
                case(0, True, False, None, None, None)
        elif hop < 4:
            case(4 - hop, hop > 0, False, ahead, from_fwd, fwd_recv)
            if hop < 3:
                case(5 + hop, False, hop > 0, behind, from_bwd, bwd_recv)
        else:
            case(0, True, True, None, None, None)

    send(0, 0, 0, x_next)
    send(0, 0, 1, x_prev)
    send(0, 0, 0, y_next)
    send(0, 0, 1, y_prev)
    send(0, 0, 1, x_next)
    send(0, 0, 0, x_prev)
    send(0, 0, 1, y_next)
    send(0, 0, 0, y_prev)
    for half in range(2):
        to_core(own, half, in_hbm(half)).start()

    for copy in load_small:
        copy.wait()
    occ_sum = column(lookup(occ_energy[...], occ_first[...]) + lookup(occ_energy[...], occ_second[...]))
    for part_of_line in range(5):
        some = pl.ds(part_of_line, 1)
        vir_sum = lookup(vir_energy[...], vir_first[some, :]) + lookup(vir_energy[...], vir_second[some, :])
        denom[:, 128 * part_of_line : 128 * part_of_line + 128] = vir_sum - occ_sum

    load_b.wait()

    @pl.loop(0, 10)
    def _(tile):
        rows = pl.ds(pl.multiple_of(tile * 128, 128), 128)
        whole = b_f32[rows, :]
        high = whole.astype(jnp.bfloat16)
        b_hi[rows, :] = high
        b_lo[rows, :] = (whole - high.astype(jnp.float32)).astype(jnp.bfloat16)

    for copy in own_copies:
        copy.wait()

    def run_events(events):
        for kind, name, detail in events:
            if kind == 0:
                gather_event(name // 4, name % 4, detail)
            else:
                reduce_event(name // 4, name % 4, kind - 1, detail)

    def body(step, carry):
        for k, events in enumerate(EVENTS):
            if events and k < len(ORDER):
                pl.when(step == k)(functools.partial(run_events, events))
        block = block_at(step)
        for half in range(2):
            arrive(block, half, 1 - core, c_recv)
        whole = a_all[block].reshape(64, 1280)
        high = whole.astype(jnp.bfloat16)
        low = (whole - high.astype(jnp.float32)).astype(jnp.bfloat16)
        dot = functools.partial(jnp.dot, preferred_element_type=jnp.float32)
        both = dot(jnp.concatenate([high, low], axis=0), b_hi[...])
        total = dot(high, b_lo[...]) + both[64:] + both[:64]
        part[block] = total.reshape(64 // PIECE, PIECE, 640)
        return carry

    def block_at(step):
        dy, dx = pick(step, [d for d, _ in ORDER]), pick(step, [d for _, d in ORDER])
        return ((y_hi + dy) % 4) * 4 + (x + dx) % 4

    lax.fori_loop(0, len(ORDER), body, 0)
    run_events(EVENTS[len(ORDER)])

    def is_pair_first(block):
        dy, dx = (block // 4 - y_hi + 4) % 4, (block % 4 - x + 4) % 4
        return functools.reduce(lambda a, b: a | b, [(dy == a) & (dx == b) for a, b in PAIR_FIRST])

    whole_sum = part[row].reshape(64, 640)
    out_ref[...] = whole_sum / denom[...]

    @pl.when(~is_pair_first(row))
    def _():
        for piece in range(64 // PIECE):
            pair_copy(row, piece).wait_recv()
        out_ref[...] = (part[row].reshape(64, 640) + from_pair[row].reshape(64, 640)) / denom[...]

    for one in sent:
        move(*one).wait_send()

    @pl.loop(0, 16)
    def _(block):
        pair_first = is_pair_first(block)
        home = block % 2 == y_lo
        for half in range(2):
            to_core(block, half, a_all.at[block, core, half]).wait_send()
        left = steps_to_go(block, 0)

        @pl.when((left != 0) & (home | ~pair_first))
        def _():
            for piece in range(64 // PIECE):
                hop_copy(block, piece, z_next, from_fwd, fwd_recv).wait_send()

        @pl.when(~home & (pair_first | (left == 0)))
        def _():
            for piece in range(64 // PIECE):
                pair_copy(block, piece).wait_send()


def per_device(
    amplitudes, integrals, occ_energy, vir_energy, occ_first, occ_second, vir_first, vir_second
):
    dma = pltpu.SemaphoreType.DMA
    f32, bf16 = jnp.float32, jnp.bfloat16
    pieces = 64 // PIECE
    chunk = pltpu.VMEM((16, pieces, PIECE, 640), f32)
    small = [array.reshape(1, -1) for array in (occ_energy, vir_energy, occ_first, occ_second)]
    small += [array.reshape(5, 128) for array in (vir_first, vir_second)]
    return pl.pallas_call(
        kernel,
        out_shape=jax.ShapeDtypeStruct((64, 640), f32),
        in_specs=[pl.BlockSpec(memory_space=pltpu.HBM)] * 8,
        out_specs=pl.BlockSpec(memory_space=pltpu.VMEM),
        scratch_shapes=[pltpu.VMEM(array.shape, array.dtype) for array in small] + [
            pltpu.VMEM((16, 2, 2, 16, 1280), f32),
            pltpu.VMEM((1280, 640), f32),
            pltpu.VMEM((1280, 640), bf16),
            pltpu.VMEM((1280, 640), bf16),
            chunk, chunk, chunk, chunk,
            pltpu.VMEM((64, 640), f32),
            dma((2,)), dma, dma((6,)), dma((30,)), dma((16, 2)),
            dma((16, 2)), dma((16, 2)),
            dma((16, pieces)), dma((16, pieces)), dma((16, pieces)), dma((16, pieces)), dma((16, pieces)),
        ],
        compiler_params=pltpu.CompilerParams(
            collective_id=0, has_side_effects=True, vmem_limit_bytes=57 * 1024 * 1024
        ),
    )(amplitudes, integrals, *small)


def solution(mesh):
    placed = (P("col", "row"), P("row", "col"), P(), P(), P("row"), P("row"), P("col"), P("col"))
    return jax.shard_map(
        per_device, mesh=mesh, in_specs=placed, out_specs=P("row", "col"), check_vma=False
    )
```

```python
import functools

import jax
import jax.numpy as jnp
from jax import lax
from jax.experimental import pallas as pl
from jax.experimental.pallas import tpu as pltpu
from jax.sharding import PartitionSpec as P

MESH = pl.DeviceIdType.MESH
ORDER = (
    ((0, 0),), ((0, 1), (0, 3),), ((0, 2),), ((1, 0), (3, 0),), ((2, 0),), ((1, 1), (1, 3),), ((3,
    1), (3, 3),), ((2, 1), (2, 3),), ((1, 2), (3, 2),), ((2, 2),),
)
PAIR_FIRST = ((2, 0), (2, 1), (2, 3), (2, 2),)
AROUND = ((0, 0), (0, 1), (0, 3), (0, 2), (1, 0), (3, 0),)
EVENTS = (
    (),
    ((1, 0, 0), (2, 0, 0), (0, 1, 1), (0, 3, 0), (0, 3, 1), (0, 1, 0), (0, 12, 0), (0, 4, 1), (1, 0, 1), (2,
     0, 1)),
    ((2, 3, 0), (1, 3, 0), (2, 1, 0), (1, 1, 0), (0, 2, 1), (0, 2, 0), (0, 4, 0), (0, 12, 1)),
    ((1, 0, 2), (2, 0, 2), (1, 2, 0), (2, 2, 0), (0, 15, 0), (2, 3, 1), (0, 7, 1), (0, 13, 0), (0, 5, 1), (2,
     1, 1), (1, 1, 1)),
    ((1, 3, 1), (2, 4, 0), (1, 4, 0), (2, 12, 0), (1, 12, 0), (0, 8, 1), (0, 8, 0), (1, 0, 3), (2, 0, 3), (0,
     5, 0), (0, 7, 0), (1, 1, 2), (0, 15, 1), (0, 13, 1)),
    ((2, 1, 2), (2, 3, 2), (1, 3, 2), (2, 4, 1), (1, 8, 0), (2, 8, 0), (1, 4, 1), (1, 2, 1), (2, 2, 1), (1,
     12, 1)),
    (),
    ((1, 0, 4), (2, 12, 1), (0, 14, 0), (1, 13, 0), (0, 6, 1), (1, 5, 0), (2, 0, 4), (2, 5, 0), (2, 13, 0),
     (1, 7, 0), (2, 7, 0), (1, 15, 0), (2, 15, 0), (1, 1, 3), (2, 1, 3), (2, 4, 2), (1, 12, 2), (1, 3, 3), (0,
     11, 0), (0, 9, 0), (0, 9, 1), (0, 11, 1), (1, 8, 1), (1, 0, 5), (1, 4, 2), (2, 3, 3), (2, 12, 2), (2, 0,
     5), (1, 2, 2), (2, 2, 2), (2, 8, 1), (1, 12, 3), (1, 5, 1), (2, 5, 1), (1, 13, 1), (0, 14, 1), (0, 6, 0),
     (2, 13, 1)),
    ((1, 15, 1), (2, 7, 1), (1, 8, 2), (1, 7, 1), (1, 1, 4), (2, 4, 3), (2, 15, 1), (2, 1, 4), (1, 9, 0), (2,
     9, 0), (1, 3, 4), (1, 4, 3), (1, 11, 0), (2, 11, 0), (1, 0, 6)),
    ((2, 12, 3), (2, 0, 6), (0, 10, 0), (0, 10, 1), (2, 8, 2), (2, 3, 4), (1, 5, 2), (1, 14, 0), (1, 6, 0),
     (2, 5, 2), (2, 6, 0), (1, 13, 2), (2, 14, 0), (2, 13, 2), (1, 2, 3), (2, 2, 3), (1, 7, 2), (2, 7, 2), (1,
     1, 5), (2, 1, 5)),
    ((2, 4, 4), (1, 15, 2), (1, 12, 4), (2, 15, 2), (1, 9, 1), (1, 10, 1), (1, 3, 5), (1, 8, 3), (1, 10, 0),
     (2, 10, 0), (1, 4, 4), (2, 10, 1), (2, 9, 1), (2, 12, 4), (1, 0, 7), (2, 0, 7), (2, 3, 5), (2, 8, 3), (2,
     13, 3), (1, 5, 3), (2, 6, 1), (1, 2, 4), (1, 7, 3), (2, 2, 4), (1, 6, 1), (1, 14, 1), (1, 11, 1), (2, 15,
     3), (1, 1, 6), (2, 5, 3), (2, 14, 1), (1, 12, 5), (1, 9, 2), (2, 4, 5), (2, 1, 6), (1, 3, 6), (1, 13, 3),
     (2, 11, 1), (1, 10, 2), (2, 10, 2), (1, 8, 4), (1, 4, 5), (2, 9, 2), (2, 3, 6), (2, 12, 5), (2, 7, 3),
     (1, 15, 3), (2, 8, 4), (1, 2, 5), (1, 5, 4), (2, 13, 4), (2, 2, 5), (2, 5, 4), (1, 3, 7), (1, 6, 2), (1,
     14, 2), (2, 14, 2), (2, 6, 2), (1, 1, 7), (2, 15, 4), (1, 11, 2), (1, 9, 3), (2, 1, 7), (1, 10, 3), (1,
     13, 4), (1, 7, 4), (2, 10, 3), (2, 3, 7), (1, 8, 5), (2, 11, 2), (1, 4, 6), (1, 12, 6), (2, 9, 3), (1,
     15, 4), (2, 4, 6), (2, 12, 6), (2, 8, 5), (2, 7, 4), (1, 2, 6), (2, 2, 6), (1, 14, 3), (2, 6, 3), (1, 6,
     3), (1, 11, 3), (2, 14, 3), (1, 10, 4), (1, 9, 4), (2, 11, 3), (2, 10, 4), (2, 4, 7), (2, 9, 4), (1, 4,
     7), (1, 12, 7), (1, 14, 4), (2, 6, 4), (1, 6, 4), (1, 11, 4), (2, 14, 4), (1, 10, 5), (2, 12, 7), (2, 11,
     4), (2, 10, 5), (1, 11, 5), (2, 9, 5), (1, 9, 5), (1, 2, 7), (2, 2, 7), (2, 11, 5)),
)
PIECE = 16


def pick(index, values):
    out = index * 0 + values[0]
    for k, value in enumerate(values):
        if value != values[0]:
            out = jnp.where(index == k, value, out)
    return out


def column(line):
    n = line.shape[1]
    down = lax.broadcasted_iota(jnp.int32, (n, n), 0)
    along = lax.broadcasted_iota(jnp.int32, (n, n), 1)
    return jnp.sum(jnp.where(down == along, line, jnp.zeros_like(line)), axis=1, keepdims=True)


def lookup(table, index):
    n, m = table.shape[0], index.shape[1]
    at = lax.broadcasted_iota(jnp.int32, (n, m), 0)
    return jnp.sum(jnp.where(at == index, table, jnp.float32(0.0)), axis=0, keepdims=True)


def kernel(
    a_hbm, b_hbm, *refs
):
    small_hbm, out_ref, small = refs[:6], refs[6], refs[7:13]
    body_of(a_hbm, b_hbm, small_hbm, out_ref, small, *refs[13:])


def body_of(
    a_hbm, b_hbm, small_hbm, out_ref, small,
    a_all, b_f32, b_hi, b_lo, part, from_fwd, from_bwd, from_pair, denom, result,
    own_sem, b_sem, small_sem, a_send, c_send, a_recv, c_recv, z_send, fwd_recv, bwd_recv, p_send, p_recv,
):
    row, col = lax.axis_index("row"), lax.axis_index("col")
    z, y_lo = row // 2, row % 2
    core, x, y_hi = col % 2, (col // 2) % 4, col // 8

    def at_col(y_to, x_to, core_to):
        return {"row": row, "col": ((y_to % 4) * 4 + x_to % 4) * 2 + core_to}

    x_next, x_prev = at_col(y_hi, x + 1, core), at_col(y_hi, x + 3, core)
    y_next, y_prev = at_col(y_hi + 1, x, core), at_col(y_hi + 3, x, core)
    other_core = at_col(y_hi, x, 1 - core)
    z_next = {"row": ((z + 1) % 8) * 2 + y_lo, "col": col}
    z_prev = {"row": ((z + 7) % 8) * 2 + y_lo, "col": col}
    y_pair = {"row": z * 2 + 1 - y_lo, "col": col}
    everyone = (x_next, x_prev, y_next, y_prev, other_core, z_next, z_prev, y_pair)

    load_b = pltpu.make_async_copy(b_hbm, b_f32, b_sem)
    load_small = [
        pltpu.make_async_copy(src, dst, small_sem.at[k]) for k, (src, dst) in enumerate(zip(small_hbm, small))
    ]
    occ_energy, vir_energy, occ_first, occ_second, vir_first, vir_second = small

    ys = [(y_hi + d) % 4 for d in range(4)]
    xs = [(x + d) % 4 for d in range(4)]

    def block_of(dy, dx):
        return ys[dy] * 4 + xs[dx]

    def in_hbm(half):
        return a_hbm.at[pl.ds(16 * half, 16), :]

    own = block_of(0, 0)
    own_copies = [
        pltpu.make_async_copy(in_hbm(half), a_all.at[own, core, half], own_sem.at[half]) for half in range(2)
    ]

    barrier = pltpu.get_barrier_semaphore()
    for device in everyone:
        pl.semaphore_signal(barrier, inc=1, device_id=device, device_id_type=MESH)
    for copy in own_copies:
        copy.start()
    for copy in load_small:
        copy.start()
    load_b.start()
    pl.semaphore_wait(barrier, len(everyone))

    sent = []

    def move(dy, dx, half, device, number):
        block = block_of(dy, dx)
        slot = a_all.at[block, core, half]
        return pltpu.make_async_remote_copy(
            src_ref=in_hbm(half) if (dy, dx) == (0, 0) else slot,
            dst_ref=slot,
            send_sem=a_send.at[number],
            recv_sem=a_recv.at[block, half],
            device_id=device,
            device_id_type=MESH,
        )

    def send(dy, dx, half, device):
        sent.append((dy, dx, half, device, len(sent)))
        move(*sent[-1]).start()

    def to_core(block, half, src):
        return pltpu.make_async_remote_copy(
            src_ref=src,
            dst_ref=a_all.at[block, core, half],
            send_sem=c_send.at[block, half],
            recv_sem=c_recv.at[block, half],
            device_id=other_core,
            device_id_type=MESH,
        )

    def arrive(block, half, whose, recv):
        slot = a_all.at[block, whose, half]
        pltpu.make_async_remote_copy(
            src_ref=slot, dst_ref=slot, send_sem=c_send.at[block, half],
            recv_sem=recv.at[block, half], device_id=other_core, device_id_type=MESH,
        ).wait_recv()

    def gather_event(dy, dx, half):
        block = block_of(dy, dx)
        arrive(block, half, core, a_recv)
        if dx == 0:
            if (dy, half) == (1, 1):
                send(dy, dx, half, y_prev)
            if (dy, half) == (3, 0):
                send(dy, dx, half, y_next)
            send(dy, dx, half, x_prev if half else x_next)
            send(dy, dx, half, x_next if half else x_prev)
        if (dx, half) == (1, 1):
            send(dy, dx, half, x_prev)
        if (dx, half) == (3, 0):
            send(dy, dx, half, x_next)
        to_core(block, half, a_all.at[block, core, half]).start()

    def hop_copy(block, piece, device, into, recv):
        return pltpu.make_async_remote_copy(
            src_ref=part.at[block, piece], dst_ref=into.at[block, piece],
            send_sem=z_send.at[block, piece], recv_sem=recv.at[block, piece],
            device_id=device, device_id_type=MESH,
        )

    def pair_copy(block, piece):
        return pltpu.make_async_remote_copy(
            src_ref=part.at[block, piece], dst_ref=from_pair.at[block, piece],
            send_sem=p_send.at[block, piece], recv_sem=p_recv.at[block, piece],
            device_id=y_pair, device_id_type=MESH,
        )

    def steps_to_go(block, parity):
        return (block // 2 - z + 8) % 8 if parity == 0 else (z - block // 2 + 8) % 8

    def reduce_event(dy, dx, parity, stage):
        block = block_of(dy, dx)
        togo = steps_to_go(block, parity)
        home = block % 2 == y_lo
        pair_first, around = (dy, dx) in PAIR_FIRST, (dy, dx) in AROUND
        ahead, behind = (z_next, z_prev) if parity == 0 else (z_prev, z_next)
        hop = stage - 1 if pair_first else stage

        def on_pieces(do):
            for piece in (parity, parity + 2):
                do(piece)

        if hop < 0:
            @pl.when(~home)
            def _():
                on_pieces(lambda piece: pair_copy(block, piece).start())
            return

        def case(left, fwd_in, bwd_in, device, into, recv):
            @pl.when((togo == left) & home if pair_first else togo == left)
            def _():
                def do(piece):
                    total = []
                    if pair_first:
                        pair_copy(block, piece).wait_recv()
                        total.append(from_pair)
                    if fwd_in:
                        hop_copy(block, piece, ahead, from_fwd, fwd_recv).wait_recv()
                        total.append(from_fwd)
                    if bwd_in:
                        hop_copy(block, piece, behind, from_bwd, bwd_recv).wait_recv()
                        total.append(from_bwd)
                    if total:
                        part[block, piece] = sum((t[block, piece] for t in total), part[block, piece])
                    if device is not None:
                        hop_copy(block, piece, device, into, recv).start()

                on_pieces(do)
                if device is None and not pair_first:
                    @pl.when(~home)
                    def _():
                        on_pieces(lambda piece: pair_copy(block, piece).start())

        if around:
            if hop < 7:
                case(7 - hop, hop > 0, False, ahead, from_fwd, fwd_recv)
            else:
                case(0, True, False, None, None, None)
        elif hop < 4:
            case(4 - hop, hop > 0, False, ahead, from_fwd, fwd_recv)
            if hop < 3:
                case(5 + hop, False, hop > 0, behind, from_bwd, bwd_recv)
        else:
            case(0, True, True, None, None, None)

    send(0, 0, 0, x_next)
    send(0, 0, 1, x_prev)
    send(0, 0, 0, y_next)
    send(0, 0, 1, y_prev)
    send(0, 0, 1, x_next)
    send(0, 0, 0, x_prev)
    send(0, 0, 1, y_next)
    send(0, 0, 0, y_prev)
    for half in range(2):
        to_core(own, half, in_hbm(half)).start()

    load_b.wait()

    @pl.loop(0, 10)
    def _(tile):
        rows = pl.ds(pl.multiple_of(tile * 128, 128), 128)
        whole = b_f32[rows, :]
        high = whole.astype(jnp.bfloat16)
        b_hi[rows, :] = high
        b_lo[rows, :] = (whole - high.astype(jnp.float32)).astype(jnp.bfloat16)

    for copy in own_copies:
        copy.wait()

    def find_denom():
        for copy in load_small:
            copy.wait()
        table = column(occ_energy[...])
        occ_sum = column(lookup(table, occ_first[...]) + lookup(table, occ_second[...]))
        table = column(vir_energy[...])
        for line in range(5):
            some = pl.ds(line, 1)
            vir_sum = lookup(table, vir_first[some, :]) + lookup(table, vir_second[some, :])
            denom[:, 128 * line : 128 * line + 128] = vir_sum - occ_sum

    def run_events(events):
        for kind, name, detail in events:
            if kind == 0:
                gather_event(name // 4, name % 4, detail)
            else:
                reduce_event(name // 4, name % 4, kind - 1, detail)

    def body(step, carry):
        for k, events in enumerate(EVENTS):
            if events and k < len(ORDER):
                pl.when(step == k)(functools.partial(run_events, events))
        dot = functools.partial(jnp.dot, preferred_element_type=jnp.float32)

        def multiply(blocks):
            for block in blocks:
                for half in range(2):
                    arrive(block, half, 1 - core, c_recv)
            whole = jnp.concatenate([a_all[block].reshape(64, 1280) for block in blocks], axis=0)
            high = whole.astype(jnp.bfloat16)
            low = (whole - high.astype(jnp.float32)).astype(jnp.bfloat16)
            both = dot(jnp.concatenate([high, low], axis=0), b_hi[...])
            rows = 64 * len(blocks)
            total = dot(high, b_lo[...]) + both[rows:] + both[:rows]
            for k, block in enumerate(blocks):
                part[block] = total[64 * k : 64 * k + 64].reshape(64 // PIECE, PIECE, 640)

        two = pick(step, [len(names) - 1 for names in ORDER]) == 1
        first, second = block_at(step, 0), block_at(step, -1)
        pl.when(step == 2)(find_denom)

        @pl.when(two)
        def _():
            multiply((first, second))

        @pl.when(~two)
        def _():
            multiply((first,))

        return carry

    def block_at(step, which):
        dy, dx = (pick(step, [names[which][axis] for names in ORDER]) for axis in range(2))
        return ((y_hi + dy) % 4) * 4 + (x + dx) % 4

    lax.fori_loop(0, len(ORDER), body, 0)
    run_events(EVENTS[len(ORDER)])

    def is_pair_first(block):
        dy, dx = (block // 4 - y_hi + 4) % 4, (block % 4 - x + 4) % 4
        return functools.reduce(lambda a, b: a | b, [(dy == a) & (dx == b) for a, b in PAIR_FIRST])

    result[...] = part[row].reshape(64, 640) / denom[...]

    @pl.when(~is_pair_first(row))
    def _():
        for piece in range(64 // PIECE):
            pair_copy(row, piece).wait_recv()
        result[...] = (part[row].reshape(64, 640) + from_pair[row].reshape(64, 640)) / denom[...]

    give_result = pltpu.make_async_copy(result, out_ref, b_sem)
    give_result.start()

    for one in sent:
        move(*one).wait_send()

    @pl.loop(0, 16)
    def _(block):
        pair_first = is_pair_first(block)
        home = block % 2 == y_lo
        for half in range(2):
            to_core(block, half, a_all.at[block, core, half]).wait_send()
        left = steps_to_go(block, 0)

        @pl.when((left != 0) & (home | ~pair_first))
        def _():
            for piece in range(64 // PIECE):
                hop_copy(block, piece, z_next, from_fwd, fwd_recv).wait_send()

        @pl.when(~home & (pair_first | (left == 0)))
        def _():
            for piece in range(64 // PIECE):
                pair_copy(block, piece).wait_send()

    give_result.wait()


def per_device(
    amplitudes, integrals, occ_energy, vir_energy, occ_first, occ_second, vir_first, vir_second
):
    dma = pltpu.SemaphoreType.DMA
    f32, bf16 = jnp.float32, jnp.bfloat16
    pieces = 64 // PIECE
    chunk = pltpu.VMEM((16, pieces, PIECE, 640), f32)
    small = [array.reshape(1, -1) for array in (occ_energy, vir_energy, occ_first, occ_second)]
    small += [array.reshape(5, 128) for array in (vir_first, vir_second)]
    return pl.pallas_call(
        kernel,
        out_shape=jax.ShapeDtypeStruct((64, 640), f32),
        in_specs=[pl.BlockSpec(memory_space=pltpu.HBM)] * 8,
        out_specs=pl.BlockSpec(memory_space=pltpu.HBM),
        scratch_shapes=[pltpu.VMEM(array.shape, array.dtype) for array in small] + [
            pltpu.VMEM((16, 2, 2, 16, 1280), f32),
            pltpu.VMEM((1280, 640), f32),
            pltpu.VMEM((1280, 640), bf16),
            pltpu.VMEM((1280, 640), bf16),
            chunk, chunk, chunk, chunk,
            pltpu.VMEM((64, 640), f32),
            pltpu.VMEM((64, 640), f32),
            dma((2,)), dma, dma((6,)), dma((30,)), dma((16, 2)),
            dma((16, 2)), dma((16, 2)),
            dma((16, pieces)), dma((16, pieces)), dma((16, pieces)), dma((16, pieces)), dma((16, pieces)),
        ],
        compiler_params=pltpu.CompilerParams(
            collective_id=0, has_side_effects=True, vmem_limit_bytes=57 * 1024 * 1024
        ),
    )(amplitudes, integrals, *small)


def solution(mesh):
    placed = (P("col", "row"), P("row", "col"), P(), P(), P("row"), P("row"), P("col"), P("col"))
    return jax.shard_map(
        per_device, mesh=mesh, in_specs=placed, out_specs=P("row", "col"), check_vma=False
    )
```

```python
import functools

import jax
import jax.numpy as jnp
from jax import lax
from jax.experimental import pallas as pl
from jax.experimental.pallas import tpu as pltpu
from jax.sharding import PartitionSpec as P

MESH = pl.DeviceIdType.MESH
ORDER = (
    ((0, 0),), ((0, 1), (0, 3),), ((0, 2),), ((1, 0), (3, 0),), ((2, 0),), ((1, 1), (1, 3),), ((3,
    1), (3, 3),), ((2, 1), (2, 3),), ((1, 2), (3, 2),), ((2, 2),),
)
PAIR_FIRST = ((2, 0), (2, 1), (2, 3), (2, 2),)
AROUND = ((0, 0), (0, 1), (0, 3), (0, 2), (1, 0), (3, 0),)
EVENTS = (
    (),
    ((1, 0, 0), (2, 0, 0), (0, 1, 1), (0, 3, 0), (0, 3, 1), (0, 1, 0), (0, 12, 0), (0, 4, 1), (1, 0, 1), (2,
     0, 1)),
    ((2, 3, 0), (1, 3, 0), (0, 2, 1), (0, 2, 0), (2, 1, 0), (1, 1, 0), (0, 4, 0), (0, 12, 1)),
    ((1, 2, 0), (2, 2, 0), (1, 0, 2), (2, 0, 2), (0, 15, 0), (0, 7, 1), (0, 13, 0), (0, 5, 1), (2, 3, 1), (2,
     1, 1), (1, 1, 1)),
    ((2, 4, 0), (1, 4, 0), (2, 12, 0), (1, 12, 0), (0, 8, 1), (1, 3, 1), (0, 8, 0), (1, 0, 3), (2, 0, 3), (0,
     5, 0), (0, 7, 0), (0, 15, 1), (0, 13, 1), (1, 1, 2)),
    ((2, 1, 2), (2, 4, 1), (2, 3, 2), (1, 3, 2), (1, 2, 1), (2, 2, 1), (1, 4, 1), (1, 8, 0), (2, 8, 0), (1,
     12, 1)),
    ((0, 14, 0), (2, 12, 1), (0, 6, 1)),
    ((1, 0, 4), (1, 13, 0), (1, 5, 0), (2, 0, 4), (2, 5, 0), (2, 13, 0), (1, 7, 0), (2, 7, 0), (1, 15, 0), (2,
     15, 0), (1, 1, 3), (2, 1, 3), (2, 4, 2), (0, 11, 0), (0, 9, 0), (0, 9, 1), (0, 11, 1), (1, 12, 2), (1, 3,
     3), (1, 8, 1), (1, 2, 2), (2, 2, 2), (1, 4, 2), (1, 0, 5), (2, 3, 3), (2, 12, 2), (2, 0, 5), (2, 8, 1),
     (1, 12, 3), (1, 5, 1), (2, 5, 1), (0, 14, 1), (0, 6, 0), (1, 13, 1), (2, 13, 1), (1, 15, 1)),
    ((2, 7, 1), (2, 4, 3), (1, 8, 2), (1, 7, 1), (2, 15, 1), (1, 1, 4), (2, 1, 4), (1, 9, 0), (2, 9, 0), (1,
     3, 4), (1, 4, 3), (1, 11, 0), (2, 11, 0), (1, 0, 6), (0, 10, 0), (0, 10, 1)),
    ((2, 12, 3), (2, 0, 6), (2, 8, 2), (2, 3, 4), (1, 2, 3), (1, 5, 2), (1, 14, 0), (1, 6, 0), (2, 2, 3), (2,
     13, 2), (2, 6, 0), (2, 14, 0), (2, 5, 2), (1, 13, 2), (2, 1, 5), (1, 8, 3), (1, 7, 2), (2, 7, 2)),
    ((2, 4, 4), (1, 12, 4), (1, 15, 2), (1, 1, 5), (2, 15, 2), (1, 9, 1), (2, 8, 3), (1, 10, 1), (1, 3, 5),
     (1, 4, 4), (2, 10, 1), (1, 10, 0), (2, 9, 1), (2, 10, 0), (2, 12, 4), (1, 0, 7), (2, 0, 7), (2, 3, 5),
     (1, 2, 4), (2, 13, 3), (2, 2, 4), (2, 6, 1), (1, 5, 3), (1, 14, 1), (1, 6, 1), (1, 7, 3), (1, 11, 1), (1,
     8, 4), (2, 14, 1), (1, 1, 6), (2, 15, 3), (2, 5, 3), (2, 4, 5), (2, 11, 1), (1, 12, 5), (1, 9, 2), (2, 1,
     6), (1, 13, 3), (1, 3, 6), (1, 10, 2), (1, 4, 5), (1, 2, 5), (2, 8, 4), (2, 10, 2), (2, 9, 2), (2, 3, 6),
     (2, 12, 5), (2, 7, 3), (1, 15, 3), (1, 5, 4), (2, 2, 5), (2, 13, 4), (1, 14, 2), (1, 6, 2), (2, 14, 2),
     (2, 6, 2), (1, 8, 5), (1, 1, 7), (2, 15, 4), (1, 11, 2), (1, 9, 3), (1, 3, 7), (2, 1, 7), (1, 13, 4), (1,
     7, 4), (2, 8, 5), (1, 10, 3), (2, 11, 2), (1, 4, 6), (2, 10, 3), (1, 12, 6), (2, 9, 3), (2, 4, 6), (1,
     15, 4), (2, 12, 6), (2, 6, 3), (2, 3, 7), (1, 2, 6), (1, 6, 3), (2, 2, 6), (2, 7, 4), (1, 14, 3), (2, 5,
     4), (2, 14, 3), (1, 11, 3), (1, 10, 4), (1, 9, 4), (2, 11, 3), (2, 10, 4), (2, 6, 4), (2, 4, 7), (1, 6,
     4), (1, 4, 7), (2, 9, 4), (1, 14, 4), (1, 12, 7), (2, 14, 4), (1, 11, 4), (2, 12, 7), (1, 10, 5), (2, 11,
     4), (2, 10, 5), (2, 9, 5), (1, 9, 5), (1, 2, 7), (1, 11, 5), (2, 2, 7), (2, 11, 5)),
)
PIECE = 16


def pick(index, values):
    out = index * 0 + values[0]
    for k, value in enumerate(values):
        if value != values[0]:
            out = jnp.where(index == k, value, out)
    return out


def column(line):
    n = line.shape[1]
    down = lax.broadcasted_iota(jnp.int32, (n, n), 0)
    along = lax.broadcasted_iota(jnp.int32, (n, n), 1)
    return jnp.sum(jnp.where(down == along, line, jnp.zeros_like(line)), axis=1, keepdims=True)


def lookup(table, index):
    n, m = table.shape[0], index.shape[1]
    at = lax.broadcasted_iota(jnp.int32, (n, m), 0)
    return jnp.sum(jnp.where(at == index, table, jnp.float32(0.0)), axis=0, keepdims=True)


def kernel(
    a_hbm, b_hbm, *refs
):
    small_hbm, out_ref, small = refs[:6], refs[6], refs[7:13]
    body_of(a_hbm, b_hbm, small_hbm, out_ref, small, *refs[13:])


def body_of(
    a_hbm, b_hbm, small_hbm, out_ref, small,
    a_all, b_f32, b_hi, b_lo, part, from_fwd, from_bwd, from_pair, denom, result,
    own_sem, b_sem, small_sem, a_send, c_send, a_recv, c_recv, z_send, fwd_recv, bwd_recv, p_send, p_recv,
):
    row, col = lax.axis_index("row"), lax.axis_index("col")
    z, y_lo = row // 2, row % 2
    core, x, y_hi = col % 2, (col // 2) % 4, col // 8

    def at_col(y_to, x_to, core_to):
        return {"row": row, "col": ((y_to % 4) * 4 + x_to % 4) * 2 + core_to}

    x_next, x_prev = at_col(y_hi, x + 1, core), at_col(y_hi, x + 3, core)
    y_next, y_prev = at_col(y_hi + 1, x, core), at_col(y_hi + 3, x, core)
    other_core = at_col(y_hi, x, 1 - core)
    z_next = {"row": ((z + 1) % 8) * 2 + y_lo, "col": col}
    z_prev = {"row": ((z + 7) % 8) * 2 + y_lo, "col": col}
    y_pair = {"row": z * 2 + 1 - y_lo, "col": col}
    everyone = (x_next, x_prev, y_next, y_prev, other_core, z_next, z_prev, y_pair)

    load_b = pltpu.make_async_copy(b_hbm, b_f32, b_sem)
    load_small = [
        pltpu.make_async_copy(src, dst, small_sem.at[k]) for k, (src, dst) in enumerate(zip(small_hbm, small))
    ]
    occ_energy, vir_energy, occ_first, occ_second, vir_first, vir_second = small

    ys = [(y_hi + d) % 4 for d in range(4)]
    xs = [(x + d) % 4 for d in range(4)]

    def block_of(dy, dx):
        return ys[dy] * 4 + xs[dx]

    def in_hbm(half):
        return a_hbm.at[pl.ds(16 * half, 16), :]

    own = block_of(0, 0)
    own_copies = [
        pltpu.make_async_copy(in_hbm(half), a_all.at[own, core, half], own_sem.at[half]) for half in range(2)
    ]

    barrier = pltpu.get_barrier_semaphore()
    for device in everyone:
        pl.semaphore_signal(barrier, inc=1, device_id=device, device_id_type=MESH)
    for copy in own_copies:
        copy.start()
    for copy in load_small:
        copy.start()
    load_b.start()
    pl.semaphore_wait(barrier, len(everyone))

    sent = []

    def move(dy, dx, half, device, number):
        block = block_of(dy, dx)
        slot = a_all.at[block, core, half]
        return pltpu.make_async_remote_copy(
            src_ref=in_hbm(half) if (dy, dx) == (0, 0) else slot,
            dst_ref=slot,
            send_sem=a_send.at[number],
            recv_sem=a_recv.at[block, half],
            device_id=device,
            device_id_type=MESH,
        )

    def send(dy, dx, half, device):
        sent.append((dy, dx, half, device, len(sent)))
        move(*sent[-1]).start()

    def to_core(block, half, src):
        return pltpu.make_async_remote_copy(
            src_ref=src,
            dst_ref=a_all.at[block, core, half],
            send_sem=c_send.at[block, half],
            recv_sem=c_recv.at[block, half],
            device_id=other_core,
            device_id_type=MESH,
        )

    def arrive(block, half, whose, recv):
        slot = a_all.at[block, whose, half]
        pltpu.make_async_remote_copy(
            src_ref=slot, dst_ref=slot, send_sem=c_send.at[block, half],
            recv_sem=recv.at[block, half], device_id=other_core, device_id_type=MESH,
        ).wait_recv()

    def gather_event(dy, dx, half):
        block = block_of(dy, dx)
        arrive(block, half, core, a_recv)
        if dx == 0:
            if (dy, half) == (1, 1):
                send(dy, dx, half, y_prev)
            if (dy, half) == (3, 0):
                send(dy, dx, half, y_next)
            send(dy, dx, half, x_prev if half else x_next)
            send(dy, dx, half, x_next if half else x_prev)
        if (dx, half) == (1, 1):
            send(dy, dx, half, x_prev)
        if (dx, half) == (3, 0):
            send(dy, dx, half, x_next)
        to_core(block, half, a_all.at[block, core, half]).start()

    def hop_copy(block, piece, device, into, recv):
        return pltpu.make_async_remote_copy(
            src_ref=part.at[block, piece], dst_ref=into.at[block, piece],
            send_sem=z_send.at[block, piece], recv_sem=recv.at[block, piece],
            device_id=device, device_id_type=MESH,
        )

    def pair_copy(block, piece):
        return pltpu.make_async_remote_copy(
            src_ref=part.at[block, piece], dst_ref=from_pair.at[block, piece],
            send_sem=p_send.at[block, piece], recv_sem=p_recv.at[block, piece],
            device_id=y_pair, device_id_type=MESH,
        )

    def steps_to_go(block, parity):
        return (block // 2 - z + 8) % 8 if parity == 0 else (z - block // 2 + 8) % 8

    def reduce_event(dy, dx, parity, stage):
        block = block_of(dy, dx)
        togo = steps_to_go(block, parity)
        home = block % 2 == y_lo
        pair_first, around = (dy, dx) in PAIR_FIRST, (dy, dx) in AROUND
        ahead, behind = (z_next, z_prev) if parity == 0 else (z_prev, z_next)
        hop = stage - 1 if pair_first else stage

        def on_pieces(do):
            for piece in (parity, parity + 2):
                do(piece)

        if hop < 0:
            @pl.when(~home)
            def _():
                on_pieces(lambda piece: pair_copy(block, piece).start())
            return

        def case(left, fwd_in, bwd_in, device, into, recv):
            @pl.when((togo == left) & home if pair_first else togo == left)
            def _():
                def do(piece):
                    total = []
                    if pair_first:
                        pair_copy(block, piece).wait_recv()
                        total.append(from_pair)
                    if fwd_in:
                        hop_copy(block, piece, ahead, from_fwd, fwd_recv).wait_recv()
                        total.append(from_fwd)
                    if bwd_in:
                        hop_copy(block, piece, behind, from_bwd, bwd_recv).wait_recv()
                        total.append(from_bwd)
                    if total:
                        part[block, piece] = sum((t[block, piece] for t in total), part[block, piece])
                    if device is not None:
                        hop_copy(block, piece, device, into, recv).start()

                on_pieces(do)
                if device is None and not pair_first:
                    @pl.when(~home)
                    def _():
                        on_pieces(lambda piece: pair_copy(block, piece).start())

        if around:
            if hop < 7:
                case(7 - hop, hop > 0, False, ahead, from_fwd, fwd_recv)
            else:
                case(0, True, False, None, None, None)
        elif hop < 4:
            case(4 - hop, hop > 0, False, ahead, from_fwd, fwd_recv)
            if hop < 3:
                case(5 + hop, False, hop > 0, behind, from_bwd, bwd_recv)
        else:
            case(0, True, True, None, None, None)

    send(0, 0, 0, x_next)
    send(0, 0, 1, x_prev)
    send(0, 0, 0, y_next)
    send(0, 0, 1, y_prev)
    send(0, 0, 1, x_next)
    send(0, 0, 0, x_prev)
    send(0, 0, 1, y_next)
    send(0, 0, 0, y_prev)
    for half in range(2):
        to_core(own, half, in_hbm(half)).start()

    load_b.wait()

    @pl.loop(0, 10)
    def _(tile):
        rows = pl.ds(pl.multiple_of(tile * 128, 128), 128)
        whole = b_f32[rows, :]
        high = whole.astype(jnp.bfloat16)
        b_hi[rows, :] = high
        b_lo[rows, :] = (whole - high.astype(jnp.float32)).astype(jnp.bfloat16)

    for copy in own_copies:
        copy.wait()

    def find_denom():
        for copy in load_small:
            copy.wait()
        table = column(occ_energy[...])
        occ_sum = column(lookup(table, occ_first[...]) + lookup(table, occ_second[...]))
        table = column(vir_energy[...])
        for line in range(5):
            some = pl.ds(line, 1)
            vir_sum = lookup(table, vir_first[some, :]) + lookup(table, vir_second[some, :])
            denom[:, 128 * line : 128 * line + 128] = vir_sum - occ_sum

    def run_events(events):
        for kind, name, detail in events:
            if kind == 0:
                gather_event(name // 4, name % 4, detail)
            else:
                reduce_event(name // 4, name % 4, kind - 1, detail)

    def body(step, carry):
        for k, events in enumerate(EVENTS):
            if events and k < len(ORDER):
                pl.when(step == k)(functools.partial(run_events, events))
        dot = functools.partial(jnp.dot, preferred_element_type=jnp.float32)

        def multiply(blocks):
            for block in blocks:
                for half in range(2):
                    arrive(block, half, 1 - core, c_recv)
            whole = jnp.concatenate([a_all[block].reshape(64, 1280) for block in blocks], axis=0)
            high = whole.astype(jnp.bfloat16)
            low = (whole - high.astype(jnp.float32)).astype(jnp.bfloat16)
            both = dot(jnp.concatenate([high, low], axis=0), b_hi[...])
            rows = 64 * len(blocks)
            total = dot(high, b_lo[...]) + both[rows:] + both[:rows]
            for k, block in enumerate(blocks):
                part[block] = total[64 * k : 64 * k + 64].reshape(64 // PIECE, PIECE, 640)

        two = pick(step, [len(names) - 1 for names in ORDER]) == 1
        first, second = block_at(step, 0), block_at(step, -1)
        pl.when(step == 2)(find_denom)

        @pl.when(two)
        def _():
            multiply((first, second))

        @pl.when(~two)
        def _():
            multiply((first,))

        return carry

    def block_at(step, which):
        dy, dx = (pick(step, [names[which][axis] for names in ORDER]) for axis in range(2))
        return ((y_hi + dy) % 4) * 4 + (x + dx) % 4

    lax.fori_loop(0, len(ORDER), body, 0)
    run_events(EVENTS[len(ORDER)])

    def is_pair_first(block):
        dy, dx = (block // 4 - y_hi + 4) % 4, (block % 4 - x + 4) % 4
        return functools.reduce(lambda a, b: a | b, [(dy == a) & (dx == b) for a, b in PAIR_FIRST])

    result[...] = part[row].reshape(64, 640) / denom[...]

    @pl.when(~is_pair_first(row))
    def _():
        for piece in range(64 // PIECE):
            pair_copy(row, piece).wait_recv()
        result[...] = (part[row].reshape(64, 640) + from_pair[row].reshape(64, 640)) / denom[...]

    give_result = pltpu.make_async_copy(result, out_ref, b_sem)
    give_result.start()

    for one in sent:
        move(*one).wait_send()

    @pl.loop(0, 16)
    def _(block):
        pair_first = is_pair_first(block)
        home = block % 2 == y_lo
        for half in range(2):
            to_core(block, half, a_all.at[block, core, half]).wait_send()
        left = steps_to_go(block, 0)

        @pl.when((left != 0) & (home | ~pair_first))
        def _():
            for piece in range(64 // PIECE):
                hop_copy(block, piece, z_next, from_fwd, fwd_recv).wait_send()

        @pl.when(~home & (pair_first | (left == 0)))
        def _():
            for piece in range(64 // PIECE):
                pair_copy(block, piece).wait_send()

    give_result.wait()


def per_device(
    amplitudes, integrals, occ_energy, vir_energy, occ_first, occ_second, vir_first, vir_second
):
    dma = pltpu.SemaphoreType.DMA
    f32, bf16 = jnp.float32, jnp.bfloat16
    pieces = 64 // PIECE
    chunk = pltpu.VMEM((16, pieces, PIECE, 640), f32)
    small = [array.reshape(1, -1) for array in (occ_energy, vir_energy, occ_first, occ_second)]
    small += [array.reshape(5, 128) for array in (vir_first, vir_second)]
    return pl.pallas_call(
        kernel,
        out_shape=jax.ShapeDtypeStruct((64, 640), f32),
        in_specs=[pl.BlockSpec(memory_space=pltpu.HBM)] * 8,
        out_specs=pl.BlockSpec(memory_space=pltpu.HBM),
        scratch_shapes=[pltpu.VMEM(array.shape, array.dtype) for array in small] + [
            pltpu.VMEM((16, 2, 2, 16, 1280), f32),
            pltpu.VMEM((1280, 640), f32),
            pltpu.VMEM((1280, 640), bf16),
            pltpu.VMEM((1280, 640), bf16),
            chunk, chunk, chunk, chunk,
            pltpu.VMEM((64, 640), f32),
            pltpu.VMEM((64, 640), f32),
            dma((2,)), dma, dma((6,)), dma((30,)), dma((16, 2)),
            dma((16, 2)), dma((16, 2)),
            dma((16, pieces)), dma((16, pieces)), dma((16, pieces)), dma((16, pieces)), dma((16, pieces)),
        ],
        compiler_params=pltpu.CompilerParams(
            collective_id=0, has_side_effects=True, vmem_limit_bytes=57 * 1024 * 1024
        ),
    )(amplitudes, integrals, *small)


def solution(mesh):
    placed = (P("col", "row"), P("row", "col"), P(), P(), P("row"), P("row"), P("col"), P("col"))
    return jax.shard_map(
        per_device, mesh=mesh, in_specs=placed, out_specs=P("row", "col"), check_vma=False
    )
```
